32 devices in a mesh: groups: 2 (over x), segment: 2 (over core), block: 8 (over z, y).
Axes of the slice: x: 2, y: 2, z: 4, core: 2. Of those that a mesh axis runs over, the one named last changes fastest.
Arguments:
- tokens: float32 [1024, 16384], P(('groups', 'segment'), 'block'), parts along dimension 0, may hold values from -32 to 32
- gains: float32 [2, 2, 16384], P('segment', None, 'block'), may hold values from 0.1 to 1.9
- right_factors: float32 [2, 2, 128, 128, 128], P('segment', None, 'block'), may hold values from -0.5 to 0.5
- left_factors: float32 [2, 2, 128, 128, 128], P('segment', None, 'block'), may hold values from -0.5 to 0.5
Outputs:
- output: float32 [1024, 16384], P(('groups', 'segment'), 'block'), parts along dimension 0
The draws below stay inside these ranges and needn't reach their ends.
There are 2 independent parts, one for each index of `groups`. The reference program is written for one: setup_inputs(seed, part) draws one part's arguments, and reference() takes and returns one part's arrays. A program takes and returns all parts, laid end to end along the dimension named above; an argument that names none is the same for every part. Nothing has to cross between parts.
All inputs are finite; a program needn't handle non-finite values.
Results may differ from the reference program's by a relative error of at most 0.0003.
Values sent between devices are 32-bit elements; how exact they have to be, the bound alone decides.
A program may use at most 64 MiB of HBM per device.

```python
import math
import jax
import jax.numpy as jnp
from jax import lax

NB = 128
BS = 128
D = 16384
ROUNDS = 2
TOKENS = 512
N_SEGMENT = 2


def draw_tokens(key, part):
    first_key, second_key = jax.random.split(key, 2)
    position = jnp.arange(D, dtype=jnp.float32) / (D - 1)
    values = jnp.clip(jax.random.normal(first_key, (TOKENS, D), jnp.float32), -5.0, 5.0)
    column_scale = 0.3 * jnp.exp(position * math.log(10.0))
    row_scale = jnp.exp(jax.random.uniform(second_key, (TOKENS, 1), jnp.float32, math.log(0.6), math.log(1.8)))
    return (values * row_scale * column_scale[None, :]).astype(jnp.float32)


def level_of(stream_key, extent, cuts, least, largest):
    loudness = 1.0
    for dim, parts in cuts:
        draws = jax.random.uniform(jax.random.fold_in(jax.random.fold_in(stream_key, 6), dim), (parts,), jnp.float32, least / len(cuts), largest / len(cuts))
        loudness = loudness * jnp.repeat(jnp.exp(draws), extent[dim] // parts).reshape((-1,) + (1,) * (len(extent) - 1 - dim))
    return loudness


def noise(key, extent, width, limit, cuts=(), kind=jnp.bfloat16):
    drawn = width * jax.random.normal(key, extent, jnp.float32)
    if cuts:
        drawn = drawn * level_of(key, extent, cuts, -0.22, 0.18)
    return jnp.clip(drawn, -limit, limit).astype(kind)


def setup_inputs(seed: int = 0, part: int = 0) -> dict:
    splits = jax.random.split(jax.random.key(seed), 5)
    own_keys = jax.random.split(jax.random.fold_in(splits[4], part), 5)
    tokens = draw_tokens(jax.random.fold_in(jax.random.fold_in(splits[4], part), 71), part)
    gains = jnp.clip(1.0 + 0.18 * jax.random.normal(splits[1], (N_SEGMENT, ROUNDS, D), jnp.float32), 0.1, 1.9)
    right_factors = noise(splits[2], (N_SEGMENT, ROUNDS, NB, BS, BS), BS ** -0.5, 0.5, ((0, 2), (2, 8)), jnp.float32)
    left_factors = noise(splits[3], (N_SEGMENT, ROUNDS, BS, NB, NB), NB ** -0.5, 0.5, ((0, 2), (2, 8)), jnp.float32)
    return {"tokens": tokens, "gains": gains, "right_factors": right_factors, "left_factors": left_factors}


epsilon = 1e-06

def one_layer(current, gain_row, right_part, left_part):
    sum_squares = lax.optimization_barrier(jnp.sum(current * current, axis=1, keepdims=True))
    normed = current * lax.rsqrt(sum_squares / D + epsilon) * gain_row[None, :]
    inner = jnp.einsum('tbi,bij->tbj', normed.reshape(-1, NB, BS), right_part, precision=lax.Precision.HIGHEST)
    mixed = jnp.einsum('tbj,jbc->tcj', inner, left_part, precision=lax.Precision.HIGHEST)
    return current + mixed.reshape(-1, D) * jax.nn.silu(normed)

def reference(tokens, gains, right_factors, left_factors):
    current = tokens
    for round_number in range(ROUNDS):
        for section in range(N_SEGMENT):
            current = one_layer(current, gains[section, round_number], right_factors[section, round_number], left_factors[section, round_number])
    return current
```

```python
import jax
import jax.numpy as jnp
from jax import lax
from jax.sharding import PartitionSpec as P

D = 16384


epsilon = 1e-06
exact = lax.Precision.HIGH


def shifted(block, axis, distance):
    devices = range(lax.axis_size(axis))
    route = [((i - distance) % len(devices), i) for i in devices]
    return lax.ppermute(block, axis, route)


def apply_layer(current, gain_row, right_part, left_part):
    blocks_here = right_part.shape[0]
    block_size = right_part.shape[1]
    width_here, token_count = current.shape
    partial_squares = jnp.sum(current * current, axis=0)
    devices = lax.axis_size("block")
    copies = jnp.broadcast_to(partial_squares, (devices, token_count))
    sum_squares = lax.all_to_all(copies, "block", 0, 0, tiled=True).sum(axis=0)
    normed = current * lax.rsqrt(sum_squares / D + epsilon)[None, :] * gain_row[:, None]
    inner = jnp.einsum(
        "bit,bij->bjt",
        normed.reshape(blocks_here, block_size, token_count),
        right_part,
        precision=exact,
    )
    combined = jnp.einsum(
        "bjt,jbc->cjt",
        lax.all_to_all(inner, "block", split_axis=1, concat_axis=0, tiled=True),
        left_part,
        precision=exact,
    )
    mixed = lax.all_to_all(combined, "block", split_axis=0, concat_axis=1, tiled=True)
    return current + mixed.reshape(width_here, token_count) * jax.nn.silu(normed)


def body(tokens, gains, right_factors, left_factors):
    current = tokens.T
    rounds = right_factors.shape[1]
    segment_index = lax.axis_index("segment")
    own = (gains[0], right_factors[0], left_factors[0])
    other = [[shifted(part[r], "segment", 1) for part in own] for r in range(rounds)]
    for layer_index in range(2 * rounds):
        section, r = layer_index % 2, layer_index // 2
        chosen = [
            jnp.where(segment_index == section, mine[r], theirs)
            for mine, theirs in zip(own, other[r])
        ]
        current = apply_layer(current, *chosen)
    return current.T


def solution(mesh):
    placed = (
        P(("groups", "segment"), "block"),
        P("segment", None, "block"),
        P("segment", None, "block", None, None),
        P("segment", None, "block", None, None),
    )
    return jax.shard_map(
        body,
        mesh=mesh,
        in_specs=placed,
        out_specs=P(("groups", "segment"), "block"),
        check_vma=False,
    )
```

```python
import functools

import jax
import jax.numpy as jnp
from jax import lax
from jax.experimental import pallas as pl
from jax.experimental.pallas import tpu as pltpu
from jax.sharding import Mesh, PartitionSpec as P

D = 16384


epsilon = 1e-06
exact = lax.Precision.HIGH


def shifted(block, axis, distance):
    devices = range(lax.axis_size(axis))
    route = [((i - distance) % len(devices), i) for i in devices]
    return lax.ppermute(block, axis, route)


def apply_layer(current, gain_row, right_part, left_part):
    blocks_here = right_part.shape[0]
    block_size = right_part.shape[1]
    width_here, token_count = current.shape
    partial_squares = jnp.sum(current * current, axis=0)
    devices = lax.axis_size("block")
    copies = jnp.broadcast_to(partial_squares, (devices, token_count))
    sum_squares = lax.all_to_all(copies, "block", 0, 0, tiled=True).sum(axis=0)
    normed = current * lax.rsqrt(sum_squares / D + epsilon)[None, :] * gain_row[:, None]
    inner = jnp.einsum(
        "bit,bij->bjt",
        normed.reshape(blocks_here, block_size, token_count),
        right_part,
        precision=exact,
    )
    combined = jnp.einsum(
        "bjt,jbc->cjt",
        lax.all_to_all(inner, "block", split_axis=1, concat_axis=0, tiled=True),
        left_part,
        precision=exact,
    )
    mixed = lax.all_to_all(combined, "block", split_axis=0, concat_axis=1, tiled=True)
    return current + mixed.reshape(width_here, token_count) * jax.nn.silu(normed)


def body(tokens, gains, right_factors, left_factors):
    current = tokens.T
    rounds = right_factors.shape[1]
    segment_index = lax.axis_index("segment")
    own = (gains[0], right_factors[0], left_factors[0])
    other = [[shifted(part[r], "segment", 1) for part in own] for r in range(rounds)]
    for layer_index in range(2 * rounds):
        section, r = layer_index % 2, layer_index // 2
        chosen = [
            jnp.where(segment_index == section, mine[r], theirs)
            for mine, theirs in zip(own, other[r])
        ]
        current = apply_layer(current, *chosen)
    return current.T


MESH = pl.DeviceIdType.MESH


def halves(value):
    high = value.astype(jnp.bfloat16)
    return high, (value - high.astype(jnp.float32)).astype(jnp.bfloat16)


def product(weight, value):
    wh, wl = halves(weight)
    vh, vl = halves(value)
    dot = functools.partial(jnp.dot, preferred_element_type=jnp.float32)
    return dot(wh, vh) + (dot(wh, vl) + dot(wl, vh))


def layers_kernel(
    hi, layers, start_ref, gain_ref, right_ref, left_ref, out_ref,
    W, N, S, A, T, M, Q,
    wsend, wrecv, fsend, frecv, qsend, qrecv, asend, arecv, msend, mrecv,
):
    x = lax.axis_index("groups")
    c = lax.axis_index("segment")
    z = lax.axis_index("hi")
    y = lax.axis_index("lo")
    here = 2 * y + c
    half = W.shape[2] // 2
    own = pl.ds(pl.multiple_of(x * half, half), half)
    steps = 2 * layers

    def peer(d):
        return (x, (c + d % 2) % 2, z, (y + d // 2) % 2)

    barrier = pltpu.get_barrier_semaphore()
    greeted = [(x, (c + dc) % 2, (z + dz) % hi, y) for dz in range(hi) for dc in range(2) if dz or dc]
    greeted += [peer(2), peer(3), (1 - x, c, z, y)]
    for device in greeted:
        pl.semaphore_signal(barrier, inc=1, device_id=device, device_id_type=MESH)
    pl.semaphore_wait(barrier, len(greeted))

    def push_copies(step, f):
        r = step // 4
        source = (right_ref, left_ref)[f]
        slot = r * 2 + f
        for dz in range(hi):
            zt = (z + dz) % hi
            for dc in range(2):
                ct = (c + dc) % 2
                rows = pl.ds(pl.multiple_of((ct * 2 + x) * half, half), half)
                src = source.at[r, rows]
                dst = W.at[step, z, own]
                if dz == 0 and dc == 0:
                    yield pltpu.make_async_copy(src, dst, wrecv.at[step, z]), False
                else:
                    yield pltpu.make_async_remote_copy(
                        src_ref=src, dst_ref=dst, send_sem=wsend.at[slot, 2 * dz + dc],
                        recv_sem=wrecv.at[step, z], device_id=(x, ct, zt, y), device_id_type=MESH,
                    ), True

    def push(step, f):
        @pl.when(c == (step // 2) % 2)
        def _():
            for copy, _ in push_copies(step, f):
                copy.start()

    def forward_copy(step, zz):
        return pltpu.make_async_remote_copy(
            src_ref=W.at[step, zz, own], dst_ref=W.at[step, zz, own],
            send_sem=fsend.at[step, zz], recv_sem=frecv.at[step, zz],
            device_id=(1 - x, c, z, y), device_id_type=MESH,
        )

    def forward(step):
        for dz in range(hi):
            zz = (z + dz) % hi
            piece = W.at[step, zz, own]
            pltpu.make_async_copy(piece, piece, wrecv.at[step, zz]).wait()
            forward_copy(step, zz).start()

    def arrived(step):
        for zz in range(hi):
            forward_copy(step, zz).wait_recv()

    def quad_copy(kind, part, d):
        if kind == "q":
            src, dst, send, recv = Q.at[part, here], Q.at[part, here], qsend.at[part, d], qrecv.at[part, d]
        else:
            target = 2 * ((y + d // 2) % 2) + (c + d % 2) % 2
            if kind == "a":
                src, dst, send, recv = S.at[part, target], A.at[:, part, here], asend, arecv
            else:
                src, dst, send, recv = T.at[part, target], M.at[part, here], msend, mrecv
            send, recv = send.at[part, d], recv.at[part, d]
            if d == 0:
                return pltpu.make_async_copy(src, dst, recv)
        return pltpu.make_async_remote_copy(
            src_ref=src, dst_ref=dst, send_sem=send, recv_sem=recv,
            device_id=peer(d), device_id_type=MESH,
        )

    push(0, 0)
    push(1, 1)
    zero = jnp.zeros((8, 128), jnp.float32)

    def start_block(b, total):
        value = start_ref[b]
        out_ref[b] = value
        return total + jnp.sum((value * value).reshape(16, 8, 128), axis=0)

    total = lax.fori_loop(0, hi * 8, start_block, zero)
    forward(0)

    def layer(l, total):
        Q[l, here] = total
        for d in (2, 3, 1):
            quad_copy("q", l, d).start()
        forward(2 * l + 1)
        for d in (2, 3, 1):
            quad_copy("q", l, d).wait()
        everyone = Q[l, 0] + Q[l, 1] + Q[l, 2] + Q[l, 3]
        sum_squares = jnp.sum(everyone, axis=0, keepdims=True)
        scale = lax.rsqrt(sum_squares / D + epsilon)
        arrived(2 * l)

        @pl.when(l + 1 < layers)
        def _():
            push(2 * l + 2, 0)

        def right_chunk(zb, carry):
            for k in range(8):
                b = zb * 8 + k
                normed = out_ref[b] * scale * gain_ref[l, b]
                N[b] = normed
                inner = product(W[2 * l, zb, k * 128:(k + 1) * 128], normed)
                tiles = inner.reshape(hi, 4, 8, 128)
                for q in range(4):
                    S[zb, q, :, k] = tiles[:, q]
            for d in (2, 3, 1, 0):
                quad_copy("a", zb, d).start()
            return carry

        lax.fori_loop(0, hi, right_chunk, 0)
        arrived(2 * l + 1)

        @pl.when(l + 1 < layers)
        def _():
            push(2 * l + 3, 1)

        for part in range(hi):
            for d in (0, 1, 2, 3):
                quad_copy("a", part, d).wait()

        def left_chunk(zj, carry):
            flat = A.at[zj].reshape(hi * 4 * 8 * 8, 128)
            for jj in range(8):
                values = flat[pl.ds(jj, 128, stride=8), :]
                mixed = product(W[2 * l + 1, zj, jj * 128:(jj + 1) * 128], values)
                tiles = mixed.reshape(hi, 4, 8, 128)
                for q in range(4):
                    T[zj, q, jj] = tiles[:, q]
            for d in (2, 3, 1, 0):
                quad_copy("m", zj, d).start()
            return carry

        lax.fori_loop(0, hi, left_chunk, 0)

        @pl.when(l + 1 < layers)
        def _():
            forward(2 * l + 2)

        for part in range(hi):
            for d in (0, 1, 2, 3):
                quad_copy("m", part, d).wait()

        flat = M.reshape(128 * hi * 8, 128)

        def close_block(b, total):
            mixed = flat[pl.ds(b, 128, stride=hi * 8), :]
            normed = N[b]
            value = out_ref[b] + mixed * (normed / (1.0 + jnp.exp(-normed)))
            out_ref[b] = value
            return total + jnp.sum((value * value).reshape(16, 8, 128), axis=0)

        return lax.fori_loop(0, hi * 8, close_block, zero)

    lax.fori_loop(0, layers, layer, total)
    for step in range(steps):
        @pl.when(c == (step // 2) % 2)
        def _():
            for copy, remote in push_copies(step, step % 2):
                if remote:
                    copy.wait_send()
        for zz in range(hi):
            forward_copy(step, zz).wait_send()


def run_layers(current, gain_rows, rights, lefts, hi, layers):
    f32 = jnp.float32
    rows = rights.shape[1] // 2
    dma = pltpu.SemaphoreType.DMA
    vmem = pl.BlockSpec(memory_space=pltpu.VMEM)
    anywhere = pl.BlockSpec(memory_space=pl.ANY)
    return pl.pallas_call(
        functools.partial(layers_kernel, hi, layers),
        out_shape=jax.ShapeDtypeStruct(current.shape, f32),
        in_specs=[vmem, vmem, anywhere, anywhere],
        out_specs=vmem,
        scratch_shapes=[
            pltpu.VMEM((2 * layers, hi, rows, 128), f32),
            pltpu.VMEM((hi * 8, 128, 128), f32),
            pltpu.VMEM((hi, 4, hi, 8, 8, 128), f32),
            pltpu.VMEM((hi, hi, 4, 8, 8, 128), f32),
            pltpu.VMEM((hi, 4, 8, hi, 8, 128), f32),
            pltpu.VMEM((hi, 4, 8, hi, 8, 128), f32),
            pltpu.VMEM((layers, 4, 8, 128), f32),
            dma((layers, 2 * hi)),
            dma((2 * layers, hi)),
            dma((2 * layers, hi)),
            dma((2 * layers, hi)),
            dma((layers, 4)),
            dma((layers, 4)),
            dma((hi, 4)),
            dma((hi, 4)),
            dma((hi, 4)),
            dma((hi, 4)),
        ],
        compiler_params=pltpu.CompilerParams(
            collective_id=0, has_side_effects=True, vmem_limit_bytes=58 * 2**20
        ),
    )(current, gain_rows, rights, lefts)


def quad_body(tokens, gains, right_factors, left_factors):
    hi = lax.axis_size("hi")
    spread = ("segment", "hi")
    rounds, here, size = right_factors.shape[1:4]
    blocks = here // 2
    rows = tokens.shape[0]
    few = rows // hi
    sent = tokens.reshape(hi, few, 2, blocks * size).transpose(2, 0, 1, 3)
    rates = gains[0].reshape(rounds, 1, 2, blocks * size).transpose(2, 1, 0, 3)
    rates = jnp.broadcast_to(rates, (2, hi, rounds, blocks * size))
    sent = jnp.concatenate([sent, rates], axis=2).reshape(2 * hi, few + rounds, blocks * size)
    came = lax.all_to_all(sent, spread, split_axis=0, concat_axis=0, tiled=True)
    came = came.reshape(2, hi, few + rounds, blocks, size)
    current = came[:, :, :few].transpose(1, 3, 4, 0, 2).reshape(hi * blocks, size, 2 * few)
    gain_rows = came[:, :, few:].transpose(2, 0, 1, 3, 4).reshape(2 * rounds, hi * blocks, size, 1)
    gain_rows = jnp.broadcast_to(gain_rows, (2 * rounds, hi * blocks, size, 2 * few))
    rights = right_factors[0].swapaxes(-1, -2).reshape(rounds, here * size, size)
    lefts = left_factors[0].swapaxes(-1, -2).reshape(rounds, here * size, size)
    current = run_layers(current, gain_rows, rights, lefts, hi, 2 * rounds)
    back = current.reshape(hi, blocks * size, 2, few).transpose(2, 0, 3, 1)
    back = back.reshape(2 * hi, few, blocks * size)
    back = lax.all_to_all(back, spread, split_axis=0, concat_axis=0, tiled=True)
    back = back.reshape(2, hi, few, blocks * size).transpose(1, 2, 0, 3)
    return back.reshape(rows, 2 * blocks * size)


def solution(mesh):
    groups, segments, devices = (mesh.shape[a] for a in ("groups", "segment", "block"))
    if (groups, segments, devices) == (2, 2, 8):
        finer = Mesh(mesh.devices.reshape(2, 2, 4, 2), ("groups", "segment", "hi", "lo"))
        block, chosen = ("hi", "lo"), quad_body
    else:
        finer, block, chosen = mesh, "block", body
    placed = (
        P(("groups", "segment"), block),
        P("segment", None, block),
        P("segment", None, block, None, None),
        P("segment", None, block, None, None),
    )
    return jax.shard_map(
        chosen,
        mesh=finer,
        in_specs=placed,
        out_specs=P(("groups", "segment"), block),
        check_vma=False,
    )
```

```python
import functools

import jax
import jax.numpy as jnp
from jax import lax
from jax.experimental import pallas as pl
from jax.experimental.pallas import tpu as pltpu
from jax.sharding import Mesh, PartitionSpec as P

D = 16384


epsilon = 1e-06
exact = lax.Precision.HIGH


def shifted(block, axis, distance):
    devices = range(lax.axis_size(axis))
    route = [((i - distance) % len(devices), i) for i in devices]
    return lax.ppermute(block, axis, route)


def apply_layer(current, gain_row, right_part, left_part):
    blocks_here = right_part.shape[0]
    block_size = right_part.shape[1]
    width_here, token_count = current.shape
    partial_squares = jnp.sum(current * current, axis=0)
    devices = lax.axis_size("block")
    copies = jnp.broadcast_to(partial_squares, (devices, token_count))
    sum_squares = lax.all_to_all(copies, "block", 0, 0, tiled=True).sum(axis=0)
    normed = current * lax.rsqrt(sum_squares / D + epsilon)[None, :] * gain_row[:, None]
    inner = jnp.einsum(
        "bit,bij->bjt",
        normed.reshape(blocks_here, block_size, token_count),
        right_part,
        precision=exact,
    )
    combined = jnp.einsum(
        "bjt,jbc->cjt",
        lax.all_to_all(inner, "block", split_axis=1, concat_axis=0, tiled=True),
        left_part,
        precision=exact,
    )
    mixed = lax.all_to_all(combined, "block", split_axis=0, concat_axis=1, tiled=True)
    return current + mixed.reshape(width_here, token_count) * jax.nn.silu(normed)


def body(tokens, gains, right_factors, left_factors):
    current = tokens.T
    rounds = right_factors.shape[1]
    segment_index = lax.axis_index("segment")
    own = (gains[0], right_factors[0], left_factors[0])
    other = [[shifted(part[r], "segment", 1) for part in own] for r in range(rounds)]
    for layer_index in range(2 * rounds):
        section, r = layer_index % 2, layer_index // 2
        chosen = [
            jnp.where(segment_index == section, mine[r], theirs)
            for mine, theirs in zip(own, other[r])
        ]
        current = apply_layer(current, *chosen)
    return current.T


MESH = pl.DeviceIdType.MESH


def halves(value):
    high = value.astype(jnp.bfloat16)
    return high, (value - high.astype(jnp.float32)).astype(jnp.bfloat16)


def product(weight, value):
    wh, wl = halves(weight)
    vh, vl = halves(value)
    dot = functools.partial(jnp.dot, preferred_element_type=jnp.float32)
    return dot(wh, vh) + (dot(wh, vl) + dot(wl, vh))


def layers_kernel(
    hi, layers, token_ref, gain_ref, right_ref, left_ref, out_ref,
    W, X, N, S, A, T, M, Q, B, G, R,
    tsend, trecv, gsend, grecv, osend, orecv,
    wsend, wrecv, fsend, frecv, qsend, qrecv, asend, arecv, msend, mrecv,
):
    x = lax.axis_index("groups")
    c = lax.axis_index("segment")
    z = lax.axis_index("hi")
    y = lax.axis_index("lo")
    here = 2 * y + c
    half = W.shape[2] // 2
    own = pl.ds(pl.multiple_of(x * half, half), half)
    steps = 2 * layers

    def peer(d):
        return (x, (c + d % 2) % 2, z, (y + d // 2) % 2)

    few, wide = B.shape[1] // 2, B.shape[2]
    G[...] = jnp.zeros(G.shape, jnp.float32)
    barrier = pltpu.get_barrier_semaphore()
    greeted = [(x, (c + dc) % 2, (z + dz) % hi, y) for dz in range(hi) for dc in range(2) if dz or dc]
    greeted += [peer(2), peer(3), (1 - x, c, z, y)]
    for device in greeted:
        pl.semaphore_signal(barrier, inc=1, device_id=device, device_id_type=MESH)
    pl.semaphore_wait(barrier, len(greeted))

    def copy_to(src, dst, send, recv, dz, dc):
        if dz == 0 and dc == 0:
            return pltpu.make_async_copy(src, dst, recv)
        return pltpu.make_async_remote_copy(
            src_ref=src, dst_ref=dst, send_sem=send, recv_sem=recv,
            device_id=(x, (c + dc) % 2, (z + dz) % hi, y), device_id_type=MESH,
        )

    others = [(dz, dc) for dz in range(hi) for dc in range(2)]

    def token_copy(dz, dc):
        zt, ct = (z + dz) % hi, (c + dc) % 2
        src = token_ref.at[pl.ds(pl.multiple_of(zt * few, few), few), pl.ds(pl.multiple_of(ct * wide, wide), wide)]
        dst = B.at[z, pl.ds(pl.multiple_of(c * few, few), few)]
        return copy_to(src, dst, tsend.at[dz, dc], trecv.at[z, c], dz, dc)

    def gain_copy(dz, dc):
        src = gain_ref.at[:, (c + dc) % 2]
        dst = G.at[c, :, pl.ds(pl.multiple_of(z * 8, 8), 8)]
        return copy_to(src, dst, gsend.at[dz, dc], grecv.at[z, c], dz, dc)

    def out_copy(dz, dc):
        zt, ct = (z + dz) % hi, (c + dc) % 2
        src = B.at[zt, pl.ds(pl.multiple_of(ct * few, few), few)]
        dst = out_ref.at[pl.ds(pl.multiple_of(z * few, few), few), pl.ds(pl.multiple_of(c * wide, wide), wide)]
        return copy_to(src, dst, osend.at[dz, dc], orecv.at[z, c], dz, dc)

    def push_copies(step, f):
        r = step // 4
        source = (right_ref, left_ref)[f]
        slot = r * 2 + f
        for dz, dc in others:
            rows = pl.ds(pl.multiple_of(((c + dc) % 2 * 2 + x) * half, half), half)
            yield copy_to(
                source.at[r, rows], W.at[step, z, own],
                wsend.at[slot, 2 * dz + dc], wrecv.at[step, z], dz, dc,
            )

    def push(step, f):
        @pl.when(c == (step // 2) % 2)
        def _():
            for copy in push_copies(step, f):
                copy.start()

    def forward_copy(step, zz):
        return pltpu.make_async_remote_copy(
            src_ref=W.at[step, zz, own], dst_ref=W.at[step, zz, own],
            send_sem=fsend.at[step, zz], recv_sem=frecv.at[step, zz],
            device_id=(1 - x, c, z, y), device_id_type=MESH,
        )

    def forward(step):
        for dz in range(hi):
            zz = (z + dz) % hi
            piece = W.at[step, zz, own]
            pltpu.make_async_copy(piece, piece, wrecv.at[step, zz]).wait()
            forward_copy(step, zz).start()

    def arrived(step):
        for zz in range(hi):
            forward_copy(step, zz).wait_recv()

    def quad_copy(kind, part, d):
        if kind == "q":
            src, dst, send, recv = Q.at[part, here], Q.at[part, here], qsend.at[part, d], qrecv.at[part, d]
        else:
            target = 2 * ((y + d // 2) % 2) + (c + d % 2) % 2
            if kind == "a":
                src, dst, send, recv = S.at[part, target], A.at[:, part, here], asend, arecv
            else:
                src, dst, send, recv = T.at[part, target], M.at[part, here], msend, mrecv
            send, recv = send.at[part, d], recv.at[part, d]
            if d == 0:
                return pltpu.make_async_copy(src, dst, recv)
        return pltpu.make_async_remote_copy(
            src_ref=src, dst_ref=dst, send_sem=send, recv_sem=recv,
            device_id=peer(d), device_id_type=MESH,
        )

    for dz, dc in others:
        gain_copy(dz, dc).start()
    for dz, dc in others:
        token_copy(dz, dc).start()
    push(0, 0)
    total = jnp.zeros((8, 128), jnp.float32)
    for dz in range(hi):
        zz = (z + dz) % hi
        for cc in range(2):
            pltpu.make_async_copy(B.at[zz, :few], B.at[zz, :few], trecv.at[zz, cc]).wait()
            piece = G.at[cc, :, pl.ds(pl.multiple_of(zz * 8, 8), 8)]
            pltpu.make_async_copy(piece, piece, grecv.at[zz, cc]).wait()
        for k in range(8):
            value = B[zz, :, k * 128:(k + 1) * 128].T
            X[zz * 8 + k] = value
            total = total + jnp.sum((value * value).reshape(16, 8, 128), axis=0)
    push(1, 1)
    for dz, dc in others:
        if dz or dc:
            token_copy(dz, dc).wait_send()
            gain_copy(dz, dc).wait_send()
    zero = jnp.zeros((8, 128), jnp.float32)
    forward(0)

    def layer(l, total):
        Q[l, here] = total
        for d in (2, 3, 1):
            quad_copy("q", l, d).start()
        @pl.when(l > 0)
        def _():
            forward(2 * l + 1)

        for zb in range(hi):
            R[zb] = G[l % 2, l // 2, zb * 8:zb * 8 + 128].T
        for d in (2, 3, 1):
            quad_copy("q", l, d).wait()
        everyone = Q[l, 0] + Q[l, 1] + Q[l, 2] + Q[l, 3]
        sum_squares = jnp.sum(everyone, axis=0, keepdims=True)
        scale = lax.rsqrt(sum_squares / D + epsilon)
        arrived(2 * l)

        @pl.when(l + 1 < layers)
        def _():
            push(2 * l + 2, 0)

        def right_chunk(zb, carry):
            for k in range(8):
                b = zb * 8 + k
                normed = X[b] * scale * R[zb, :, k:k + 1]
                N[b] = normed
                inner = product(W[2 * l, zb, k * 128:(k + 1) * 128], normed)
                tiles = inner.reshape(hi, 4, 8, 128)
                for q in range(4):
                    S[zb, q, :, k] = tiles[:, q]
            for d in (2, 3, 1, 0):
                quad_copy("a", zb, d).start()
            return carry

        lax.fori_loop(0, hi, right_chunk, 0)

        @pl.when(l == 0)
        def _():
            forward(1)

        arrived(2 * l + 1)

        @pl.when(l + 1 < layers)
        def _():
            push(2 * l + 3, 1)

        for part in range(hi):
            for d in (0, 1, 2, 3):
                quad_copy("a", part, d).wait()

        def left_chunk(zj, carry):
            flat = A.at[zj].reshape(hi * 4 * 8 * 8, 128)
            for jj in range(8):
                values = flat[pl.ds(jj, 128, stride=8), :]
                mixed = product(W[2 * l + 1, zj, jj * 128:(jj + 1) * 128], values)
                tiles = mixed.reshape(hi, 4, 8, 128)
                for q in range(4):
                    T[zj, q, jj] = tiles[:, q]
            for d in (2, 3, 1, 0):
                quad_copy("m", zj, d).start()
            return carry

        lax.fori_loop(0, hi, left_chunk, 0)

        @pl.when(l + 1 < layers)
        def _():
            forward(2 * l + 2)

        for part in range(hi):
            for d in (0, 1, 2, 3):
                quad_copy("m", part, d).wait()

        flat = M.reshape(128 * hi * 8, 128)

        def close_block(b, total):
            mixed = flat[pl.ds(b, 128, stride=hi * 8), :]
            normed = N[b]
            value = X[b] + mixed * (normed / (1.0 + jnp.exp(-normed)))
            X[b] = value
            return total + jnp.sum((value * value).reshape(16, 8, 128), axis=0)

        return lax.fori_loop(0, hi * 8, close_block, zero)

    lax.fori_loop(0, layers, layer, total)
    for dz in range(hi):
        zz = (z + dz) % hi
        for k in range(8):
            B[zz, :, k * 128:(k + 1) * 128] = X[zz * 8 + k].T
        for dc in range(2):
            out_copy(dz, dc).start()
    for step in range(steps):
        @pl.when(c == (step // 2) % 2)
        def _():
            for i, copy in enumerate(push_copies(step, step % 2)):
                if i:
                    copy.wait_send()
        for zz in range(hi):
            forward_copy(step, zz).wait_send()
    for dz, dc in others:
        if dz or dc:
            out_copy(dz, dc).wait_send()
    for zz in range(hi):
        for cc in range(2):
            piece = out_ref.at[zz * few:(zz + 1) * few, cc * wide:(cc + 1) * wide]
            pltpu.make_async_copy(piece, piece, orecv.at[zz, cc]).wait()


def quad_body(tokens, gains, right_factors, left_factors):
    f32 = jnp.float32
    hi = lax.axis_size("hi")
    rounds, here, size = right_factors.shape[1:4]
    layers = 2 * rounds
    rows = here * size // 2
    few = tokens.shape[0] // hi
    rates = gains[0].reshape(rounds, 2, here // 2, size)
    rights = right_factors[0].swapaxes(-1, -2).reshape(rounds, here * size, size)
    lefts = left_factors[0].swapaxes(-1, -2).reshape(rounds, here * size, size)
    dma = pltpu.SemaphoreType.DMA
    anywhere = pl.BlockSpec(memory_space=pl.ANY)
    return pl.pallas_call(
        functools.partial(layers_kernel, hi, layers),
        out_shape=jax.ShapeDtypeStruct(tokens.shape, f32),
        in_specs=[anywhere] * 4,
        out_specs=anywhere,
        scratch_shapes=[
            pltpu.VMEM((2 * layers, hi, rows, 128), f32),
            pltpu.VMEM((hi * 8, 128, 128), f32),
            pltpu.VMEM((hi * 8, 128, 128), f32),
            pltpu.VMEM((hi, 4, hi, 8, 8, 128), f32),
            pltpu.VMEM((hi, hi, 4, 8, 8, 128), f32),
            pltpu.VMEM((hi, 4, 8, hi, 8, 128), f32),
            pltpu.VMEM((hi, 4, 8, hi, 8, 128), f32),
            pltpu.VMEM((layers, 4, 8, 128), f32),
            pltpu.VMEM((hi, 2 * few, rows), f32),
            pltpu.VMEM((2, rounds, 128 + 8 * hi, 128), f32),
            pltpu.VMEM((hi, 128, 128), f32),
            *[dma((hi, 2))] * 6,
            dma((layers, 2 * hi)),
            dma((2 * layers, hi)),
            dma((2 * layers, hi)),
            dma((2 * layers, hi)),
            dma((layers, 4)),
            dma((layers, 4)),
            dma((hi, 4)),
            dma((hi, 4)),
            dma((hi, 4)),
            dma((hi, 4)),
        ],
        compiler_params=pltpu.CompilerParams(
            collective_id=0, has_side_effects=True, vmem_limit_bytes=58 * 2**20
        ),
    )(tokens, rates, rights, lefts)


def solution(mesh):
    groups, segments, devices = (mesh.shape[a] for a in ("groups", "segment", "block"))
    if (groups, segments, devices) == (2, 2, 8):
        finer = Mesh(mesh.devices.reshape(2, 2, 4, 2), ("groups", "segment", "hi", "lo"))
        block, chosen = ("hi", "lo"), quad_body
    else:
        finer, block, chosen = mesh, "block", body
    placed = (
        P(("groups", "segment"), block),
        P("segment", None, block),
        P("segment", None, block, None, None),
        P("segment", None, block, None, None),
    )
    return jax.shard_map(
        chosen,
        mesh=finer,
        in_specs=placed,
        out_specs=P(("groups", "segment"), block),
        check_vma=False,
    )
```

```python
import functools

import jax
import jax.numpy as jnp
from jax import lax
from jax.experimental import pallas as pl
from jax.experimental.pallas import tpu as pltpu
from jax.sharding import Mesh, PartitionSpec as P

D = 16384


epsilon = 1e-06
exact = lax.Precision.HIGH


def shifted(block, axis, distance):
    devices = range(lax.axis_size(axis))
    route = [((i - distance) % len(devices), i) for i in devices]
    return lax.ppermute(block, axis, route)


def apply_layer(current, gain_row, right_part, left_part):
    blocks_here = right_part.shape[0]
    block_size = right_part.shape[1]
    width_here, token_count = current.shape
    partial_squares = jnp.sum(current * current, axis=0)
    devices = lax.axis_size("block")
    copies = jnp.broadcast_to(partial_squares, (devices, token_count))
    sum_squares = lax.all_to_all(copies, "block", 0, 0, tiled=True).sum(axis=0)
    normed = current * lax.rsqrt(sum_squares / D + epsilon)[None, :] * gain_row[:, None]
    inner = jnp.einsum(
        "bit,bij->bjt",
        normed.reshape(blocks_here, block_size, token_count),
        right_part,
        precision=exact,
    )
    combined = jnp.einsum(
        "bjt,jbc->cjt",
        lax.all_to_all(inner, "block", split_axis=1, concat_axis=0, tiled=True),
        left_part,
        precision=exact,
    )
    mixed = lax.all_to_all(combined, "block", split_axis=0, concat_axis=1, tiled=True)
    return current + mixed.reshape(width_here, token_count) * jax.nn.silu(normed)


def body(tokens, gains, right_factors, left_factors):
    current = tokens.T
    rounds = right_factors.shape[1]
    segment_index = lax.axis_index("segment")
    own = (gains[0], right_factors[0], left_factors[0])
    other = [[shifted(part[r], "segment", 1) for part in own] for r in range(rounds)]
    for layer_index in range(2 * rounds):
        section, r = layer_index % 2, layer_index // 2
        chosen = [
            jnp.where(segment_index == section, mine[r], theirs)
            for mine, theirs in zip(own, other[r])
        ]
        current = apply_layer(current, *chosen)
    return current.T


MESH = pl.DeviceIdType.MESH


def halves(value):
    high = value.astype(jnp.bfloat16)
    return high, (value - high.astype(jnp.float32)).astype(jnp.bfloat16)


def product(weight, value):
    wh, wl = halves(weight)
    vh, vl = halves(value)
    dot = functools.partial(jnp.dot, preferred_element_type=jnp.float32)
    return dot(wh, vh) + (dot(wh, vl) + dot(wl, vh))


def layers_kernel(
    hi, layers, token_ref, gain_ref, right_ref, left_ref, out_ref,
    W, X, N, S, A, T, M, Q, B, G, R,
    tsend, trecv, gsend, grecv, osend, orecv,
    wsend, wrecv, fsend, frecv, qsend, qrecv, asend, arecv, msend, mrecv,
):
    x = lax.axis_index("groups")
    c = lax.axis_index("segment")
    z = lax.axis_index("hi")
    y = lax.axis_index("lo")
    here = 2 * y + c
    half = W.shape[2] // 2
    own = pl.ds(pl.multiple_of(x * half, half), half)
    steps = 2 * layers

    def peer(d):
        return (x, (c + d % 2) % 2, z, (y + d // 2) % 2)

    few, wide = B.shape[1] // 2, B.shape[2]
    G[...] = jnp.zeros(G.shape, jnp.float32)
    barrier = pltpu.get_barrier_semaphore()
    greeted = [(x, (c + dc) % 2, (z + dz) % hi, y) for dz in range(hi) for dc in range(2) if dz or dc]
    greeted += [peer(2), peer(3), (1 - x, c, z, y)]
    for device in greeted:
        pl.semaphore_signal(barrier, inc=1, device_id=device, device_id_type=MESH)
    pl.semaphore_wait(barrier, len(greeted))

    def copy_to(src, dst, send, recv, dz, dc):
        if dz == 0 and dc == 0:
            return pltpu.make_async_copy(src, dst, recv)
        return pltpu.make_async_remote_copy(
            src_ref=src, dst_ref=dst, send_sem=send, recv_sem=recv,
            device_id=(x, (c + dc) % 2, (z + dz) % hi, y), device_id_type=MESH,
        )

    others = [(dz, dc) for dz in range(hi) for dc in range(2)]

    def token_copy(dz, dc):
        zt, ct = (z + dz) % hi, (c + dc) % 2
        src = token_ref.at[pl.ds(pl.multiple_of(zt * few, few), few), pl.ds(pl.multiple_of(ct * wide, wide), wide)]
        dst = B.at[z, pl.ds(pl.multiple_of(c * few, few), few)]
        return copy_to(src, dst, tsend.at[dz, dc], trecv.at[z, c], dz, dc)

    def gain_copy(dz, dc):
        src = gain_ref.at[:, (c + dc) % 2]
        dst = G.at[c, z, :, :8]
        return copy_to(src, dst, gsend.at[dz, dc], grecv.at[z, c], dz, dc)

    def out_copy(dz, dc):
        zt, ct = (z + dz) % hi, (c + dc) % 2
        src = B.at[zt, pl.ds(pl.multiple_of(ct * few, few), few)]
        dst = out_ref.at[pl.ds(pl.multiple_of(z * few, few), few), pl.ds(pl.multiple_of(c * wide, wide), wide)]
        return copy_to(src, dst, osend.at[dz, dc], orecv.at[z, c], dz, dc)

    def push_copies(step, f, chosen=others):
        r = step // 4
        source = (right_ref, left_ref)[f]
        slot = r * 2 + f
        for dz, dc in chosen:
            rows = pl.ds(pl.multiple_of(((c + dc) % 2 * 2 + x) * half, half), half)
            yield copy_to(
                source.at[r, rows], W.at[step, z, own],
                wsend.at[slot, 2 * dz + dc], wrecv.at[step, z], dz, dc,
            )

    def push(step, f):
        @pl.when(c == (step // 2) % 2)
        def _():
            for copy in push_copies(step, f):
                copy.start()

    def forward_copy(step, zz):
        return pltpu.make_async_remote_copy(
            src_ref=W.at[step, zz, own], dst_ref=W.at[step, zz, own],
            send_sem=fsend.at[step, zz], recv_sem=frecv.at[step, zz],
            device_id=(1 - x, c, z, y), device_id_type=MESH,
        )

    def forward_from(step, zz):
        piece = W.at[step, zz, own]
        pltpu.make_async_copy(piece, piece, wrecv.at[step, zz]).wait()
        forward_copy(step, zz).start()

    def forward(step):
        for dz in range(hi):
            forward_from(step, (z + dz) % hi)

    def arrived(step):
        for zz in range(hi):
            forward_copy(step, zz).wait_recv()

    def quad_copy(kind, part, d):
        if kind == "q":
            src, dst, send, recv = Q.at[part, here], Q.at[part, here], qsend.at[part, d], qrecv.at[part, d]
        else:
            target = 2 * ((y + d // 2) % 2) + (c + d % 2) % 2
            if kind == "a":
                src, dst, send, recv = S.at[part, target], A.at[:, part, here], asend, arecv
            else:
                src, dst, send, recv = T.at[part, target], M.at[part, here], msend, mrecv
            send, recv = send.at[part, d], recv.at[part, d]
            if d == 0:
                return pltpu.make_async_copy(src, dst, recv)
        return pltpu.make_async_remote_copy(
            src_ref=src, dst_ref=dst, send_sem=send, recv_sem=recv,
            device_id=peer(d), device_id_type=MESH,
        )

    def squares(value):
        return jnp.sum((value * value).reshape(16, 8, 128), axis=0)

    def right_block(l, zb, k, value):
        scaled = value * R[zb, :, k:k + 1]
        N[zb * 8 + k] = scaled
        inner = product(W[2 * l, zb, k * 128:(k + 1) * 128], scaled)
        tiles = inner.reshape(hi, 4, 8, 128)
        for q in range(4):
            S[zb, q, :, k] = tiles[:, q]

    def send_right(zb):
        for d in (2, 3, 1, 0):
            quad_copy("a", zb, d).start()

    def send_squares(l, total):
        Q[l, here] = total
        for d in (2, 3, 1):
            quad_copy("q", l, d).start()

    for dz, dc in others:
        gain_copy(dz, dc).start()
    for dz in range(hi):
        for dc in range(2):
            token_copy(dz, dc).start()

        @pl.when(c == 0)
        def _():
            for copy in push_copies(0, 0, others[2 * dz:2 * dz + 2]):
                copy.start()

    zero = jnp.zeros((8, 128), jnp.float32)
    total = zero
    for dz in range(hi):
        zz = (z + dz) % hi
        for cc in range(2):
            piece = B.at[zz, cc * few:(cc + 1) * few]
            pltpu.make_async_copy(piece, piece, trecv.at[zz, cc]).wait()
            piece = G.at[cc, zz, :, :8]
            pltpu.make_async_copy(piece, piece, grecv.at[zz, cc]).wait()
        for k in range(8):
            value = B[zz, :, k * 128:(k + 1) * 128].T
            X[zz * 8 + k] = value
            total = total + squares(value)
        forward_from(0, zz)
    send_squares(0, total)
    push(1, 1)

    def first_chunk(dz, carry):
        zz = lax.rem(z + dz, hi)
        R[zz] = G[0, zz, 0].T
        forward_copy(0, zz).wait_recv()
        for k in range(8):
            right_block(0, zz, k, X[zz * 8 + k])
        send_right(zz)
        return carry

    lax.fori_loop(0, hi, first_chunk, 0)
    for dz, dc in others:
        if dz or dc:
            token_copy(dz, dc).wait_send()
            gain_copy(dz, dc).wait_send()

    def layer(l, last):
        for d in (2, 3, 1):
            quad_copy("q", l, d).wait()
        everyone = Q[l, 0] + Q[l, 1] + Q[l, 2] + Q[l, 3]
        sum_squares = jnp.sum(everyone, axis=0, keepdims=True)
        scale = lax.rsqrt(sum_squares / D + epsilon)
        forward(2 * l + 1)
        arrived(2 * l + 1)
        if not last:
            push(2 * l + 2, 0)
        for part in range(hi):
            for d in (0, 1, 2, 3):
                quad_copy("a", part, d).wait()

        def left_chunk(zj, carry):
            flat = A.at[zj].reshape(hi * 4 * 8 * 8, 128)
            for jj in range(8):
                values = flat[pl.ds(jj, 128, stride=8), :] * scale
                mixed = product(W[2 * l + 1, zj, jj * 128:(jj + 1) * 128], values)
                tiles = mixed.reshape(hi, 4, 8, 128)
                for q in range(4):
                    T[zj, q, jj] = tiles[:, q]
            for d in (2, 3, 1, 0):
                quad_copy("m", zj, d).start()
            return carry

        lax.fori_loop(0, hi, left_chunk, 0)
        if not last:
            push(2 * l + 3, 1)
            forward(2 * l + 2)
        for part in range(hi):
            for d in (0, 1, 2, 3):
                quad_copy("m", part, d).wait()
        flat = M.reshape(128 * hi * 8, 128)

        def closed(b):
            mixed = flat[pl.ds(b, 128, stride=hi * 8), :]
            normed = N[b] * scale
            return X[b] + mixed * (normed / (1.0 + jnp.exp(-normed)))

        if last:
            for dz in range(hi):
                zz = (z + dz) % hi
                for k in range(8):
                    B[zz, :, k * 128:(k + 1) * 128] = closed(zz * 8 + k).T
                for dc in range(2):
                    out_copy(dz, dc).start()
            return
        arrived(2 * l + 2)

        def next_chunk(dz, total):
            zb = lax.rem(z + dz, hi)
            R[zb] = G[(l + 1) % 2, zb, (l + 1) // 2].T
            for k in range(8):
                value = closed(zb * 8 + k)
                X[zb * 8 + k] = value
                total = total + squares(value)
                right_block(l + 1, zb, k, value)
            send_right(zb)
            return total

        send_squares(l + 1, lax.fori_loop(0, hi, next_chunk, zero))

    def inner_layer(l, carry):
        layer(l, False)
        return carry

    lax.fori_loop(0, layers - 1, inner_layer, 0)
    layer(layers - 1, True)
    for step in range(steps):
        @pl.when(c == (step // 2) % 2)
        def _():
            for i, copy in enumerate(push_copies(step, step % 2)):
                if i:
                    copy.wait_send()
        for zz in range(hi):
            forward_copy(step, zz).wait_send()
    for dz, dc in others:
        if dz or dc:
            out_copy(dz, dc).wait_send()
    for zz in range(hi):
        for cc in range(2):
            piece = out_ref.at[zz * few:(zz + 1) * few, cc * wide:(cc + 1) * wide]
            pltpu.make_async_copy(piece, piece, orecv.at[zz, cc]).wait()


def quad_body(tokens, gains, right_factors, left_factors):
    f32 = jnp.float32
    hi = lax.axis_size("hi")
    rounds, here, size = right_factors.shape[1:4]
    layers = 2 * rounds
    rows = here * size // 2
    few = tokens.shape[0] // hi
    rates = gains[0].reshape(rounds, 2, here // 2, size)
    rights = right_factors[0].swapaxes(-1, -2).reshape(rounds, here * size, size)
    lefts = left_factors[0].swapaxes(-1, -2).reshape(rounds, here * size, size)
    dma = pltpu.SemaphoreType.DMA
    anywhere = pl.BlockSpec(memory_space=pl.ANY)
    return pl.pallas_call(
        functools.partial(layers_kernel, hi, layers),
        out_shape=jax.ShapeDtypeStruct(tokens.shape, f32),
        in_specs=[anywhere] * 4,
        out_specs=anywhere,
        scratch_shapes=[
            pltpu.VMEM((2 * layers, hi, rows, 128), f32),
            pltpu.VMEM((hi * 8, 128, 128), f32),
            pltpu.VMEM((hi * 8, 128, 128), f32),
            pltpu.VMEM((hi, 4, hi, 8, 8, 128), f32),
            pltpu.VMEM((hi, hi, 4, 8, 8, 128), f32),
            pltpu.VMEM((hi, 4, 8, hi, 8, 128), f32),
            pltpu.VMEM((hi, 4, 8, hi, 8, 128), f32),
            pltpu.VMEM((layers, 4, 8, 128), f32),
            pltpu.VMEM((hi, 2 * few, rows), f32),
            pltpu.VMEM((2, hi, rounds, 128, 128), f32),
            pltpu.VMEM((hi, 128, 128), f32),
            *[dma((hi, 2))] * 6,
            dma((layers, 2 * hi)),
            dma((2 * layers, hi)),
            dma((2 * layers, hi)),
            dma((2 * layers, hi)),
            dma((layers, 4)),
            dma((layers, 4)),
            dma((hi, 4)),
            dma((hi, 4)),
            dma((hi, 4)),
            dma((hi, 4)),
        ],
        compiler_params=pltpu.CompilerParams(
            collective_id=0, has_side_effects=True, vmem_limit_bytes=58 * 2**20
        ),
    )(tokens, rates, rights, lefts)


def solution(mesh):
    groups, segments, devices = (mesh.shape[a] for a in ("groups", "segment", "block"))
    if (groups, segments, devices) == (2, 2, 8):
        finer = Mesh(mesh.devices.reshape(2, 2, 4, 2), ("groups", "segment", "hi", "lo"))
        block, chosen = ("hi", "lo"), quad_body
    else:
        finer, block, chosen = mesh, "block", body
    placed = (
        P(("groups", "segment"), block),
        P("segment", None, block),
        P("segment", None, block, None, None),
        P("segment", None, block, None, None),
    )
    return jax.shard_map(
        chosen,
        mesh=finer,
        in_specs=placed,
        out_specs=P(("groups", "segment"), block),
        check_vma=False,
    )
```

```python
import functools

import jax
import jax.numpy as jnp
from jax import lax
from jax.experimental import pallas as pl
from jax.experimental.pallas import tpu as pltpu
from jax.sharding import Mesh, PartitionSpec as P

D = 16384


epsilon = 1e-06
exact = lax.Precision.HIGH


def shifted(block, axis, distance):
    devices = range(lax.axis_size(axis))
    route = [((i - distance) % len(devices), i) for i in devices]
    return lax.ppermute(block, axis, route)


def apply_layer(current, gain_row, right_part, left_part):
    blocks_here = right_part.shape[0]
    block_size = right_part.shape[1]
    width_here, token_count = current.shape
    partial_squares = jnp.sum(current * current, axis=0)
    devices = lax.axis_size("block")
    copies = jnp.broadcast_to(partial_squares, (devices, token_count))
    sum_squares = lax.all_to_all(copies, "block", 0, 0, tiled=True).sum(axis=0)
    normed = current * lax.rsqrt(sum_squares / D + epsilon)[None, :] * gain_row[:, None]
    inner = jnp.einsum(
        "bit,bij->bjt",
        normed.reshape(blocks_here, block_size, token_count),
        right_part,
        precision=exact,
    )
    combined = jnp.einsum(
        "bjt,jbc->cjt",
        lax.all_to_all(inner, "block", split_axis=1, concat_axis=0, tiled=True),
        left_part,
        precision=exact,
    )
    mixed = lax.all_to_all(combined, "block", split_axis=0, concat_axis=1, tiled=True)
    return current + mixed.reshape(width_here, token_count) * jax.nn.silu(normed)


def body(tokens, gains, right_factors, left_factors):
    current = tokens.T
    rounds = right_factors.shape[1]
    segment_index = lax.axis_index("segment")
    own = (gains[0], right_factors[0], left_factors[0])
    other = [[shifted(part[r], "segment", 1) for part in own] for r in range(rounds)]
    for layer_index in range(2 * rounds):
        section, r = layer_index % 2, layer_index // 2
        chosen = [
            jnp.where(segment_index == section, mine[r], theirs)
            for mine, theirs in zip(own, other[r])
        ]
        current = apply_layer(current, *chosen)
    return current.T


MESH = pl.DeviceIdType.MESH


def halves(value):
    high = value.astype(jnp.bfloat16)
    return high, (value - high.astype(jnp.float32)).astype(jnp.bfloat16)


def product(weight, value):
    wh, wl = halves(weight)
    vh, vl = halves(value)
    dot = functools.partial(jnp.dot, preferred_element_type=jnp.float32)
    return dot(wh, vh) + (dot(wh, vl) + dot(wl, vh))


def layers_kernel(
    hi, layers, token_ref, gain_ref, right_ref, left_ref, out_ref,
    W, X, N, S, A, T, M, Q, B, G, R,
    tsend, trecv, gsend, grecv, osend, orecv,
    wsend, wrecv, fsend, frecv, qsend, qrecv, asend, arecv, msend, mrecv,
):
    x = lax.axis_index("groups")
    c = lax.axis_index("segment")
    z = lax.axis_index("hi")
    y = lax.axis_index("lo")
    here = 2 * y + c
    half = W.shape[2] // 2
    own = pl.ds(pl.multiple_of(x * half, half), half)
    steps = 2 * layers

    def peer(d):
        return (x, (c + d % 2) % 2, z, (y + d // 2) % 2)

    few, wide = B.shape[1] // 2, B.shape[2]
    G[...] = jnp.zeros(G.shape, jnp.float32)
    barrier = pltpu.get_barrier_semaphore()
    greeted = [(x, (c + dc) % 2, (z + dz) % hi, y) for dz in range(hi) for dc in range(2) if dz or dc]
    greeted += [peer(2), peer(3), (1 - x, c, z, y)]
    for device in greeted:
        pl.semaphore_signal(barrier, inc=1, device_id=device, device_id_type=MESH)
    pl.semaphore_wait(barrier, len(greeted))

    def copy_to(src, dst, send, recv, dz, dc):
        if dz == 0 and dc == 0:
            return pltpu.make_async_copy(src, dst, recv)
        return pltpu.make_async_remote_copy(
            src_ref=src, dst_ref=dst, send_sem=send, recv_sem=recv,
            device_id=(x, (c + dc) % 2, (z + dz) % hi, y), device_id_type=MESH,
        )

    others = [(dz, dc) for dz in range(hi) for dc in range(2)]

    def token_copy(dz, dc):
        zt, ct = (z + dz) % hi, (c + dc) % 2
        src = token_ref.at[pl.ds(pl.multiple_of(zt * few, few), few), pl.ds(pl.multiple_of(ct * wide, wide), wide)]
        dst = B.at[z, pl.ds(pl.multiple_of(c * few, few), few)]
        return copy_to(src, dst, tsend.at[dz, dc], trecv.at[z, c], dz, dc)

    def gain_copy(dz, dc):
        src = gain_ref.at[:, (c + dc) % 2]
        dst = G.at[c, z, :, :8]
        return copy_to(src, dst, gsend.at[dz, dc], grecv.at[z, c], dz, dc)

    def out_copy(dz, dc):
        zt, ct = (z + dz) % hi, (c + dc) % 2
        src = B.at[zt, pl.ds(pl.multiple_of(ct * few, few), few)]
        dst = out_ref.at[pl.ds(pl.multiple_of(z * few, few), few), pl.ds(pl.multiple_of(c * wide, wide), wide)]
        return copy_to(src, dst, osend.at[dz, dc], orecv.at[z, c], dz, dc)

    def push_copies(step, f, chosen=others):
        r = step // 4
        source = (right_ref, left_ref)[f]
        slot = r * 2 + f
        for dz, dc in chosen:
            rows = pl.ds(pl.multiple_of(((c + dc) % 2 * 2 + x) * half, half), half)
            yield copy_to(
                source.at[r, rows], W.at[step, z, own],
                wsend.at[slot, 2 * dz + dc], wrecv.at[step, z], dz, dc,
            )

    def push(step, f):
        @pl.when(c == (step // 2) % 2)
        def _():
            for copy in push_copies(step, f):
                copy.start()

    def push_some(step, f, dz):
        for i in range(hi):
            @pl.when((dz == i) & (step < steps) & (c == (step // 2) % 2))
            def _():
                for copy in push_copies(step, f, others[2 * i:2 * i + 2]):
                    copy.start()

    def forward_copy(step, zz):
        return pltpu.make_async_remote_copy(
            src_ref=W.at[step, zz, own], dst_ref=W.at[step, zz, own],
            send_sem=fsend.at[step, zz], recv_sem=frecv.at[step, zz],
            device_id=(1 - x, c, z, y), device_id_type=MESH,
        )

    def forward_from(step, zz):
        piece = W.at[step, zz, own]
        pltpu.make_async_copy(piece, piece, wrecv.at[step, zz]).wait()
        forward_copy(step, zz).start()

    def forward(step):
        for dz in range(hi):
            forward_from(step, (z + dz) % hi)

    def arrived(step):
        for zz in range(hi):
            forward_copy(step, zz).wait_recv()

    def quad_copy(kind, part, d):
        if kind == "q":
            src, dst, send, recv = Q.at[part, here], Q.at[part, here], qsend.at[part, d], qrecv.at[part, d]
        else:
            target = 2 * ((y + d // 2) % 2) + (c + d % 2) % 2
            if kind == "a":
                src, dst, send, recv = S.at[part, target], A.at[:, part, here], asend, arecv
            else:
                src, dst, send, recv = T.at[part, target], M.at[part, here], msend, mrecv
            send, recv = send.at[part, d], recv.at[part, d]
            if d == 0:
                return pltpu.make_async_copy(src, dst, recv)
        return pltpu.make_async_remote_copy(
            src_ref=src, dst_ref=dst, send_sem=send, recv_sem=recv,
            device_id=peer(d), device_id_type=MESH,
        )

    def squares(value):
        return jnp.sum((value * value).reshape(16, 8, 128), axis=0)

    def right_block(l, zb, k, value):
        scaled = value * R[zb, :, k:k + 1]
        N[zb * 8 + k] = scaled
        inner = product(W[2 * l, zb, k * 128:(k + 1) * 128], scaled)
        tiles = inner.reshape(hi, 4, 8, 128)
        for q in range(4):
            S[zb, q, :, k] = tiles[:, q]

    def send_right(zb):
        for d in (2, 3, 1, 0):
            quad_copy("a", zb, d).start()

    def send_squares(l, total):
        Q[l, here] = total
        for d in (2, 3, 1):
            quad_copy("q", l, d).start()

    for dz, dc in others:
        gain_copy(dz, dc).start()
    for dz in range(hi):
        for dc in range(2):
            token_copy(dz, dc).start()

        @pl.when(c == 0)
        def _():
            for copy in push_copies(0, 0, others[2 * dz:2 * dz + 2]):
                copy.start()

    zero = jnp.zeros((8, 128), jnp.float32)
    total = zero
    for dz in range(hi):
        zz = (z + dz) % hi
        for cc in range(2):
            piece = B.at[zz, cc * few:(cc + 1) * few]
            pltpu.make_async_copy(piece, piece, trecv.at[zz, cc]).wait()
            piece = G.at[cc, zz, :, :8]
            pltpu.make_async_copy(piece, piece, grecv.at[zz, cc]).wait()
        for k in range(8):
            value = B[zz, :, k * 128:(k + 1) * 128].T
            X[zz * 8 + k] = value
            total = total + squares(value)
        forward_from(0, zz)
    send_squares(0, total)
    push(1, 1)

    def first_chunk(dz, carry):
        zz = lax.rem(z + dz, hi)
        R[zz] = G[0, zz, 0].T
        forward_copy(0, zz).wait_recv()
        for k in range(8):
            right_block(0, zz, k, X[zz * 8 + k])
        send_right(zz)
        push_some(2, 0, dz)
        return carry

    lax.fori_loop(0, hi, first_chunk, 0)
    for dz, dc in others:
        if dz or dc:
            token_copy(dz, dc).wait_send()
            gain_copy(dz, dc).wait_send()

    def layer(l, last):
        for d in (2, 3, 1):
            quad_copy("q", l, d).wait()
        everyone = Q[l, 0] + Q[l, 1] + Q[l, 2] + Q[l, 3]
        sum_squares = jnp.sum(everyone, axis=0, keepdims=True)
        scale = lax.rsqrt(sum_squares / D + epsilon)
        if not last:
            @pl.when(l == 0)
            def _():
                forward(1)
        arrived(2 * l + 1)
        for part in range(hi):
            for d in (0, 1, 2, 3):
                quad_copy("a", part, d).wait()

        if not last:
            forward(2 * l + 2)

        def left_chunk(zj, carry):
            flat = A.at[zj].reshape(hi * 4 * 8 * 8, 128)
            for jj in range(8):
                values = flat[pl.ds(jj, 128, stride=8), :] * scale
                mixed = product(W[2 * l + 1, zj, jj * 128:(jj + 1) * 128], values)
                tiles = mixed.reshape(hi, 4, 8, 128)
                for q in range(4):
                    T[zj, q, jj] = tiles[:, q]
            for d in (2, 3, 1, 0):
                quad_copy("m", zj, d).start()
            if not last:
                push_some(2 * l + 3, 1, zj)
            return carry

        lax.fori_loop(0, hi, left_chunk, 0)
        for part in range(hi):
            for d in (0, 1, 2, 3):
                quad_copy("m", part, d).wait()
        flat = M.reshape(128 * hi * 8, 128)

        def closed(b):
            mixed = flat[pl.ds(b, 128, stride=hi * 8), :]
            normed = N[b] * scale
            return X[b] + mixed * (normed / (1.0 + jnp.exp(-normed)))

        if last:
            for dz in range(hi):
                zz = (z + dz) % hi
                for k in range(8):
                    B[zz, :, k * 128:(k + 1) * 128] = closed(zz * 8 + k).T
                for dc in range(2):
                    out_copy(dz, dc).start()
            return
        arrived(2 * l + 2)
        forward(2 * l + 3)

        def next_chunk(dz, total):
            zb = lax.rem(z + dz, hi)
            R[zb] = G[(l + 1) % 2, zb, (l + 1) // 2].T
            for k in range(8):
                value = closed(zb * 8 + k)
                X[zb * 8 + k] = value
                total = total + squares(value)
                right_block(l + 1, zb, k, value)
            send_right(zb)
            push_some(2 * l + 4, 0, dz)
            return total

        send_squares(l + 1, lax.fori_loop(0, hi, next_chunk, zero))

    def inner_layer(l, carry):
        layer(l, False)
        return carry

    lax.fori_loop(0, layers - 1, inner_layer, 0)
    layer(layers - 1, True)
    for step in range(steps):
        @pl.when(c == (step // 2) % 2)
        def _():
            for i, copy in enumerate(push_copies(step, step % 2)):
                if i:
                    copy.wait_send()
        for zz in range(hi):
            forward_copy(step, zz).wait_send()
    for dz, dc in others:
        if dz or dc:
            out_copy(dz, dc).wait_send()
    for zz in range(hi):
        for cc in range(2):
            piece = out_ref.at[zz * few:(zz + 1) * few, cc * wide:(cc + 1) * wide]
            pltpu.make_async_copy(piece, piece, orecv.at[zz, cc]).wait()


def quad_body(tokens, gains, right_factors, left_factors):
    f32 = jnp.float32
    hi = lax.axis_size("hi")
    rounds, here, size = right_factors.shape[1:4]
    layers = 2 * rounds
    rows = here * size // 2
    few = tokens.shape[0] // hi
    rates = gains[0].reshape(rounds, 2, here // 2, size)
    rights = right_factors[0].swapaxes(-1, -2).reshape(rounds, here * size, size)
    lefts = left_factors[0].swapaxes(-1, -2).reshape(rounds, here * size, size)
    dma = pltpu.SemaphoreType.DMA
    anywhere = pl.BlockSpec(memory_space=pl.ANY)
    return pl.pallas_call(
        functools.partial(layers_kernel, hi, layers),
        out_shape=jax.ShapeDtypeStruct(tokens.shape, f32),
        in_specs=[anywhere] * 4,
        out_specs=anywhere,
        scratch_shapes=[
            pltpu.VMEM((2 * layers, hi, rows, 128), f32),
            pltpu.VMEM((hi * 8, 128, 128), f32),
            pltpu.VMEM((hi * 8, 128, 128), f32),
            pltpu.VMEM((hi, 4, hi, 8, 8, 128), f32),
            pltpu.VMEM((hi, hi, 4, 8, 8, 128), f32),
            pltpu.VMEM((hi, 4, 8, hi, 8, 128), f32),
            pltpu.VMEM((hi, 4, 8, hi, 8, 128), f32),
            pltpu.VMEM((layers, 4, 8, 128), f32),
            pltpu.VMEM((hi, 2 * few, rows), f32),
            pltpu.VMEM((2, hi, rounds, 128, 128), f32),
            pltpu.VMEM((hi, 128, 128), f32),
            *[dma((hi, 2))] * 6,
            dma((layers, 2 * hi)),
            dma((2 * layers, hi)),
            dma((2 * layers, hi)),
            dma((2 * layers, hi)),
            dma((layers, 4)),
            dma((layers, 4)),
            dma((hi, 4)),
            dma((hi, 4)),
            dma((hi, 4)),
            dma((hi, 4)),
        ],
        compiler_params=pltpu.CompilerParams(
            collective_id=0, has_side_effects=True, vmem_limit_bytes=58 * 2**20
        ),
    )(tokens, rates, rights, lefts)


def solution(mesh):
    groups, segments, devices = (mesh.shape[a] for a in ("groups", "segment", "block"))
    if (groups, segments, devices) == (2, 2, 8):
        finer = Mesh(mesh.devices.reshape(2, 2, 4, 2), ("groups", "segment", "hi", "lo"))
        block, chosen = ("hi", "lo"), quad_body
    else:
        finer, block, chosen = mesh, "block", body
    placed = (
        P(("groups", "segment"), block),
        P("segment", None, block),
        P("segment", None, block, None, None),
        P("segment", None, block, None, None),
    )
    return jax.shard_map(
        chosen,
        mesh=finer,
        in_specs=placed,
        out_specs=P(("groups", "segment"), block),
        check_vma=False,
    )
```
